32 devices in a mesh: expert: 8 (over z, y), dp: 4 (over x, core).
Axes of the slice: x: 2, y: 2, z: 4, core: 2. Of those that a mesh axis runs over, the one named last changes fastest.
Arguments:
- tokens: bfloat16 [1024, 2048], P(('dp', 'expert')), may hold values from -6 to 6
- expert_ids: int32 [1024, 2], P(('dp', 'expert')), may hold values from 0 to 7, all different within a row; in each aligned block of 32 rows (0 to 31, 32 to 63, ...) at most 16 rows name the same one
- gates: float32 [1024, 2], P(('dp', 'expert')), may hold values from 0.1 to 1
- valid: int32 [1024], P(('dp', 'expert')), may hold values 0 or 1
- w_in: bfloat16 [8, 2048, 8192], P('expert', None, 'dp'), may hold values from -0.125 to 0.125
- w_out: bfloat16 [8, 8192, 2048], P('expert', 'dp'), may hold values from -0.0625 to 0.0625
- up_proj: bfloat16 [2048, 8192], P(None, 'expert'), may hold values from -0.125 to 0.125
- down_proj: bfloat16 [8192, 2048], P('expert'), may hold values from -0.0625 to 0.0625
Outputs:
- grad_up: float32 [2048, 8192], P('dp', 'expert')
- grad_down: float32 [8192, 2048], P('expert', 'dp')
The draws below stay inside these ranges and needn't reach their ends.
Inputs may be any that keep to these rules, and one draw needn't show every extreme that they name: `expert_ids`: the two experts of a token differ; among the 32 rows of one device no expert is named more than 16 times, a bound that some block reaches.
All inputs are finite; a program needn't handle non-finite values. No bound on the sum of `valid` on one device may be relied on, other than what follows from the above.
Results may differ from the reference program's by a relative error of at most 0.017.
Values may be sent and summed in bfloat16 or wider, within the bound.
No kernel may reach another device: no remote copies, remote signals or barrier semaphores. Data moves between devices by JAX's collectives and lax.ppermute only.
A program may use at most 128 MiB of HBM per device.

```python
import math
import jax
import jax.numpy as jnp
import numpy as np
from jax import lax

D = 2048
FF = 8192
SFF = 8192
TOK_DEV = 32
EXPERTS = 8
CAP = 16
TOKENS = 1024
N_EXPERT = 8
N_DP = 4


def set_ends(array, own_key, low, top_value):
    longest = array.shape.index(max(array.shape))
    spots = []
    for shift in (0, 1):
        where = [jax.random.randint(jax.random.fold_in(own_key, axis), (), 0, length) for axis, length in enumerate(array.shape)]
        where[longest] = (where[longest] + shift) % array.shape[longest]
        spots.append(tuple(where))
    return array.at[spots[0]].set(low).at[spots[1]].set(top_value)


def levels(rng, extent, pieces, low, high):
    gain, own = 1.0, jax.random.fold_in(rng, 6)
    for axis_at, blocks in pieces:
        steps = jnp.exp(jax.random.uniform(jax.random.fold_in(own, axis_at), (blocks,), jnp.float32, low / len(pieces), high / len(pieces)))
        gain = gain * jnp.repeat(steps, extent[axis_at] // blocks).reshape([-1 if axis == axis_at else 1 for axis in range(len(extent))])
    return gain


def routed_block(rng, own, number, rows, number_of, top, limit, skew):
    ranking = jax.random.permutation(rng, number_of)
    heavy_load, common = shares(number_of, rows * top, limit, skew, True), shares(number_of, rows * top, limit, skew, False)
    places = jnp.arange(number_of)

    def named(sizes, rotation):
        used = int((sizes > 0).sum())
        fixed = max(1, used // 4)
        moved = fixed + (places - fixed + rotation * (used - fixed)) % max(1, number_of - fixed)
        return jnp.zeros((number_of,), jnp.int32).at[ranking[jnp.where(places < fixed, places, moved)]].set(jnp.asarray(sizes, jnp.int32))

    sizes = jnp.where(number % 4 == 0, named(heavy_load, number // 4), named(common, number - number // 4 - 1))
    mixed = jax.random.permutation(jax.random.fold_in(own, 3), number_of)
    source_of, sink = mixed[0:number_of // 2 * 2:2], mixed[1:number_of // 2 * 2:2]
    margin = jnp.minimum(sizes[source_of] - 1, limit - sizes[sink]) // 2
    margin = jnp.where((source_of == ranking[0]) | (sink == ranking[0]) | (sizes[sink] == 0), 0, jnp.maximum(margin, 0))
    moved = jax.random.randint(jax.random.fold_in(own, 4), (number_of // 2,), 0, 1 << 20) % (margin + 1)
    sizes = sizes.at[source_of].add(-moved).at[sink].add(moved)
    labels = jnp.searchsorted(jnp.cumsum(sizes), jnp.arange(rows * top), side="right").astype(jnp.int32)
    table = labels.reshape(top, rows).T
    table = table[jax.random.permutation(jax.random.fold_in(own, 1), rows)]
    rotation = jax.random.randint(jax.random.fold_in(own, 2), (rows, 1), 0, top)
    return jnp.take_along_axis(table, (jnp.arange(top)[None, :] + rotation) % top, axis=1)


def shares(count, total, bound, lean, full):
    weights = [(1 << 20) // math.isqrt(standing ** lean) + 1 for standing in range(1, count + 1)]
    largest = bound if full else min(bound, max(-(-total // count), total * weights[0] // sum(weights)))
    least = 1 if total - largest >= count - 1 else 0
    given, rest = [largest] + [least] * (count - 1), total - largest - least * (count - 1)
    while rest > 0:
        free = [i for i in range(1, count) if given[i] < largest] or [i for i in range(1, count) if given[i] < bound]
        pool, remaining = sum([weights[i] for i in free]), rest
        for i in free:
            addition = min(bound - given[i], max(1, remaining * weights[i] // pool), rest)
            given[i] = given[i] + addition
            rest = rest - addition
    return np.array(given)


def centred(stream_key, extent, width, reach, shards=(), kind=jnp.bfloat16):
    factor_of = levels(stream_key, extent, shards, -0.22, 0.18) if shards else 1.0
    result = jax.random.normal(stream_key, extent, jnp.float32) * width * factor_of
    return jnp.minimum(jnp.maximum(result, -reach), reach).astype(kind)


def setup_inputs(seed: int = 0) -> dict:
    seeds = jax.random.split(jax.random.key(seed), 9)
    tokens = centred(seeds[0], (TOKENS, D), 1.0, 6.0, ((0, 32),))
    expert_ids_keys = jax.random.split(jax.random.fold_in(seeds[1], 1), TOKENS // TOK_DEV)
    expert_ids_turns = jax.random.permutation(jax.random.fold_in(seeds[1], 3), TOKENS // TOK_DEV)
    expert_ids = jax.vmap(lambda own, number: routed_block(jax.random.fold_in(seeds[1], 2), own, number, TOK_DEV, EXPERTS, 2, CAP, 2))(expert_ids_keys, expert_ids_turns).reshape((TOKENS, 2))
    gates = jnp.clip(0.1 + 0.9 * jax.random.uniform(seeds[2], (TOKENS, 2), jnp.float32) ** levels(seeds[2], (TOKENS, 2), ((0, 32),), -0.2, 0.2), 0.1, 1.0)
    valid = set_ends((jax.random.randint(seeds[3], (TOKENS,), 0, 4) < 3).astype(jnp.int32), jax.random.fold_in(seeds[3], 1), 0, 1)
    w_in = centred(seeds[4], (EXPERTS, D, FF), D ** -0.5, 0.125, ((0, 8), (2, 4)))
    w_out = centred(seeds[5], (EXPERTS, FF, D), FF ** -0.5, 0.0625, ((0, 8), (1, 4)))
    up_proj = centred(seeds[6], (D, SFF), D ** -0.5, 0.125, ((1, 8),))
    down_proj = centred(seeds[7], (SFF, D), SFF ** -0.5, 0.0625, ((0, 8),))
    return dict(tokens=tokens, expert_ids=expert_ids, gates=gates, valid=valid, w_in=w_in, w_out=w_out, up_proj=up_proj, down_proj=down_proj)


def silu_grad(preact):
    sigmoid = jax.nn.sigmoid(preact)
    return sigmoid * (1.0 + preact * (1.0 - sigmoid))

def reference(tokens, expert_ids, gates, valid, w_in, w_out, up_proj, down_proj):
    n_blocks = TOKENS // TOK_DEV
    block_ids = expert_ids.reshape(n_blocks, TOK_DEV * 2)
    expert_hot = (block_ids[:, :, None] == jnp.arange(EXPERTS, dtype=jnp.int32)[None, None, :]).astype(jnp.int32)
    ranks = lax.optimization_barrier(jnp.sum((jnp.cumsum(expert_hot, axis=1) - 1) * expert_hot, axis=2))
    sources = jnp.arange(n_blocks, dtype=jnp.int32)[:, None]
    slot_rows = (sources * CAP + ranks).reshape(-1).astype(jnp.int32)
    token_index = jnp.repeat(jnp.arange(TOKENS, dtype=jnp.int32), 2)
    flat_ids = expert_ids.reshape(-1).astype(jnp.int32)
    table = jnp.full((EXPERTS, n_blocks * CAP), TOKENS, jnp.int32).at[flat_ids, slot_rows].set(token_index)
    gate_table = jnp.zeros((EXPERTS, n_blocks * CAP), jnp.float32).at[flat_ids, slot_rows].set(gates.reshape(-1))
    padded = jnp.concatenate([tokens, jnp.zeros((1, D), tokens.dtype)], axis=0)
    block_width = FF // N_DP

    def expert_step(target, inputs):
        slot_index, gate_col, inner_weight, outer_weight = inputs
        gathered = padded[slot_index]
        teacher_hidden = jax.nn.relu(jnp.dot(gathered, inner_weight, preferred_element_type=jnp.float32)).astype(jnp.bfloat16)
        summed = jnp.zeros((gathered.shape[0], D), jnp.float32)
        for part_index in range(N_DP):
            partial_value = jnp.dot(teacher_hidden[:, part_index * block_width:(part_index + 1) * block_width], outer_weight[part_index * block_width:(part_index + 1) * block_width], preferred_element_type=jnp.float32).astype(jnp.bfloat16)
            summed = summed + lax.optimization_barrier(partial_value).astype(jnp.float32)
        expert_out = lax.optimization_barrier(summed.astype(jnp.bfloat16)).astype(jnp.float32)
        return (target.at[slot_index].add(gate_col[:, None] * expert_out), None)
    target, _ = lax.scan(expert_step, jnp.zeros((TOKENS + 1, D), jnp.float32), (table, gate_table, w_in, w_out))
    target = target[:TOKENS]
    preact = jnp.dot(tokens, up_proj, preferred_element_type=jnp.float32)
    student_hidden = jax.nn.silu(preact).astype(jnp.bfloat16)
    student_block = SFF // N_EXPERT
    student_out = jnp.zeros((TOKENS, D), jnp.float32)
    for part_index in range(N_EXPERT):
        partial_value = jnp.dot(student_hidden[:, part_index * student_block:(part_index + 1) * student_block], down_proj[part_index * student_block:(part_index + 1) * student_block], preferred_element_type=jnp.float32).astype(jnp.bfloat16)
        student_out = student_out + lax.optimization_barrier(partial_value).astype(jnp.float32)
    scale = 1.0 / jnp.sqrt(jnp.float32(TOKENS))
    out_grad = (valid[:, None].astype(jnp.float32) * (student_out - target) * scale).astype(jnp.bfloat16)
    grad_down = lax.dot_general(student_hidden, out_grad, (((0,), (0,)), ((), ())), preferred_element_type=jnp.float32)
    back_hidden = lax.dot_general(out_grad, down_proj, (((1,), (1,)), ((), ())), preferred_element_type=jnp.float32)
    hidden_grad = (back_hidden * silu_grad(preact)).astype(jnp.bfloat16)
    grad_up = lax.dot_general(tokens, hidden_grad, (((0,), (0,)), ((), ())), preferred_element_type=jnp.float32)
    return (grad_up, grad_down)
```

```python
import jax
import jax.numpy as jnp
from jax import lax
from jax.sharding import PartitionSpec as P


BF = jnp.bfloat16
F32 = jnp.float32


def silu_grad(preact):
    sigmoid = jax.nn.sigmoid(preact)
    return sigmoid * (1.0 + preact * (1.0 - sigmoid))


def swap(x, axis, k):
    return lax.ppermute(x, axis, [(i, i ^ k) for i in range(lax.axis_size(axis))])


def minor_size(n):
    m = 1
    while 8 * m * m <= n:
        m *= 2
    return m


def dot(a, b, dims):
    return lax.dot_general(a, b, (dims, ((), ())), preferred_element_type=F32)


def gather_expert(x, ny, nz):
    col = jnp.concatenate([x] + [swap(x, "expert", kz * ny) for kz in range(1, nz)], 0)
    return [col] + [swap(col, "expert", ky) for ky in range(1, ny)]


def gather_dp(x, n_d):
    out = [None] * n_d
    out[0] = x
    for j in range(2, n_d, 2):
        out[j] = swap(x, "dp", j)
    for j in range(0, n_d, 2):
        out[j + 1] = swap(out[j], "dp", 1)
    return out


def columns_dp(x, n_d):
    d = lax.axis_index("dp")
    width = x.shape[1] // n_d
    cut = lambda j: lax.dynamic_slice_in_dim(x, (d ^ j) * width, width, 1)
    out = [None] * n_d
    out[0] = cut(0)
    pass_on = [cut(1)]
    for j in range(2, n_d, 2):
        both = swap(jnp.concatenate([cut(j), cut(j + 1)], 0), "dp", j)
        out[j] = both[: x.shape[0]]
        pass_on.append(both[x.shape[0] :])
    passed = swap(jnp.concatenate(pass_on, 0), "dp", 1)
    for j in range(0, n_d, 2):
        out[j + 1] = passed[j // 2 * x.shape[0] : (j // 2 + 1) * x.shape[0]]
    return out


def per_device(tokens, expert_ids, gates, valid, w_in, w_out, up_proj, down_proj):
    n_e = lax.axis_size("expert")
    n_d = lax.axis_size("dp")
    ny = minor_size(n_e)
    nz = n_e // ny
    tok_count, width = tokens.shape
    capacity = 4 * tok_count // n_e
    slot_width = n_e * capacity
    s = lax.axis_index("expert")

    flat_ids = expert_ids.reshape(-1)
    relative = flat_ids ^ s
    place = (relative % ny) * nz + relative // ny
    expert_hot = (place[:, None] == jnp.arange(n_e, dtype=jnp.int32)[None, :]).astype(jnp.int32)
    ranks = jnp.sum((jnp.cumsum(expert_hot, axis=0) - 1) * expert_hot, axis=1)
    slots = place * capacity + ranks
    slot_hot = (slots[:, None] == jnp.arange(slot_width, dtype=jnp.int32)[None, :]).astype(BF)
    paired = slot_hot.reshape(tok_count, 2, slot_width)
    placing = paired[:, 0, :] + paired[:, 1, :]
    outgoing = dot(placing, tokens, ((0,), (0,))).astype(BF)

    returned = []
    for ky in range(ny):
        arrived = []
        for kz in range(nz):
            p = ky * nz + kz
            block = outgoing[p * capacity : (p + 1) * capacity]
            arrived.append(swap(block, "expert", kz * ny + ky) if p else block)
        rows = jnp.concatenate(gather_dp(jnp.concatenate(arrived, 0), n_d), 0)
        hidden = jax.nn.relu(dot(rows, w_in[0], ((1,), (0,)))).astype(BF)
        part = dot(hidden, w_out[0], ((1,), (0,))).astype(BF)
        part = part.reshape(n_d // 2, 2, nz * capacity, width)
        other = swap(part[:, 1], "dp", 1)
        pair = part[:, 0].astype(F32) + other.astype(F32)
        total = pair[0]
        for j in range(1, n_d // 2):
            total = total + swap(pair[j].astype(BF), "dp", 2 * j).astype(F32)
        expert_out = total.astype(BF)
        for kz in range(nz):
            block = expert_out[kz * capacity : (kz + 1) * capacity]
            returned.append(swap(block, "expert", kz * ny + ky) if kz + ky else block)
    picked = dot(slot_hot, jnp.concatenate(returned, 0), ((1,), (0,))).reshape(tok_count, 2, width)
    target = gates[:, 0:1] * picked[:, 0, :] + gates[:, 1:2] * picked[:, 1, :]

    group_tokens = jnp.concatenate(gather_expert(tokens, ny, nz), 0)
    token_cols = columns_dp(group_tokens, n_d)
    preact = dot(group_tokens, up_proj, ((1,), (0,)))
    student_hidden = jax.nn.silu(preact).astype(BF)
    hidden_all = gather_dp(student_hidden, n_d)
    partial_out = dot(student_hidden, down_proj, ((1,), (0,))).astype(BF).reshape(ny, nz * tok_count, width)
    column = partial_out[0].astype(F32)
    for ky in range(1, ny):
        column = column + swap(partial_out[ky], "expert", ky).astype(F32)
    column = column.reshape(nz, tok_count, width)
    student_out = column[0]
    for kz in range(1, nz):
        student_out = student_out + swap(column[kz].astype(BF), "expert", kz * ny).astype(F32)

    scale = 1.0 / jnp.sqrt(jnp.float32(tok_count * n_e * n_d))
    out_grad = (valid[:, None].astype(F32) * (student_out - target) * scale).astype(BF)

    chunk = nz * tok_count
    grad_up = grad_down = None
    for ky, group_grad in enumerate(gather_expert(out_grad, ny, nz)):
        mine = slice(ky * chunk, (ky + 1) * chunk)
        grad_cols = jnp.concatenate(columns_dp(group_grad, n_d), 0)
        back = dot(group_grad, down_proj, ((1,), (1,)))
        hidden_grad = (back * silu_grad(preact[mine])).astype(BF)
        grads = jnp.concatenate(gather_dp(hidden_grad, n_d), 0)
        up = dot(jnp.concatenate([t[mine] for t in token_cols], 0), grads, ((0,), (0,)))
        down = dot(jnp.concatenate([h[mine] for h in hidden_all], 0), grad_cols, ((0,), (0,)))
        grad_up = up if ky == 0 else grad_up + up
        grad_down = down if ky == 0 else grad_down + down
    return (grad_up, grad_down)


def solution(mesh):
    return jax.shard_map(
        per_device,
        mesh=mesh,
        in_specs=(
            P(("dp", "expert"), None),
            P(("dp", "expert"), None),
            P(("dp", "expert"), None),
            P(("dp", "expert")),
            P("expert", None, "dp"),
            P("expert", "dp", None),
            P(None, "expert"),
            P("expert", None),
        ),
        out_specs=(P("dp", "expert"), P("expert", "dp")),
        check_vma=False,
    )
```
